512 devices in a mesh: dp: 8 (over y, core), ctx: 64 (over z, x).
Axes of the slice: x: 4, y: 4, z: 16, core: 2. Of those that a mesh axis runs over, the one named last changes fastest.
Arguments:
- query_in: bfloat16 [8, 8192, 1792], P('dp', 'ctx'), may hold values from -8 to 8
- key_in: bfloat16 [8, 8192, 256], P('dp', 'ctx'), may hold values from -4 to 4
- value_input: bfloat16 [8, 8192, 256], P('dp', 'ctx'), may hold values from -4 to 4
- output_gradient: bfloat16 [8, 8192, 1792], P('dp', 'ctx'), may hold values from -5 to 5
- doc_ids: int32 [8, 8192], P('dp', 'ctx'), may hold values from 0 to 1, as said below
- query_bias: float32 [1792], replicated, may hold values from -2 to 2
Outputs:
- attended: bfloat16 [8, 8192, 1792], P('dp', 'ctx')
- grad_query: bfloat16 [8, 8192, 1792], P('dp', 'ctx')
- key_gradient: bfloat16 [8, 8192, 256], P('dp', 'ctx')
- value_gradient: bfloat16 [8, 8192, 256], P('dp', 'ctx')
- grad_bias: float32 [1792], replicated
The draws below stay inside these ranges and needn't reach their ends.
Inputs may be any that keep to these rules, and one draw needn't show every extreme that they name: `doc_ids`: ids never fall along a sequence; each of the 2 documents of a sequence holds 2048 to 6144 tokens, and together they fill all 8192 tokens.
All inputs are finite; a program needn't handle non-finite values.
Results may differ from the reference program's by a relative error of at most 0.019.
Values may be sent and summed in bfloat16 or wider, within the bound.
A program may use at most 64 MiB of HBM per device.

```python
import math
import jax
import jax.numpy as jnp
from jax import lax

QUERY_HEADS = 14
KEY_VALUE_HEADS = 2
HEAD_SIZE = 128
GROUP_SIZE = 7
BLK = 128
WB = 16
SEQUENCE_LENGTH = 8192
BATCH_COUNT = 8
DOC_MOST = 6144


def draw_query_in(key, part):
    value_rows = jnp.clip(jax.random.normal(jax.random.fold_in(key, 23), (BATCH_COUNT, SEQUENCE_LENGTH, QUERY_HEADS * HEAD_SIZE), jnp.float32), -4.0, 4.0)
    return value_rows.astype(jnp.bfloat16)


def draw_key_in(key, part):
    value_rows = jnp.clip(jax.random.normal(jax.random.fold_in(key, 33), (BATCH_COUNT, SEQUENCE_LENGTH, KEY_VALUE_HEADS * HEAD_SIZE), jnp.float32), -4.0, 4.0)
    return value_rows.astype(jnp.bfloat16)


def draw_doc_ids(key, part):
    first_length = jax.random.randint(jax.random.fold_in(key, 4471), (BATCH_COUNT, 1), SEQUENCE_LENGTH - DOC_MOST, DOC_MOST + 1)
    positions = jnp.arange(SEQUENCE_LENGTH, dtype=jnp.int32)[None, :]
    return (positions >= first_length).astype(jnp.int32)


def shard_levels(stream_key, shape, split, low, top_value):
    level = 1.0
    for axis_at, blocks in split:
        heights = jax.random.uniform(jax.random.fold_in(jax.random.fold_in(stream_key, 6), axis_at), (blocks,), jnp.float32, low / len(split), top_value / len(split))
        level = level * jnp.repeat(jnp.exp(heights), shape[axis_at] // blocks).reshape((-1,) + (1,) * (len(shape) - 1 - axis_at))
    return level


def scatter_about(stream_key, shape, width, bound, pieces=(), kind=jnp.bfloat16):
    gain = shard_levels(stream_key, shape, pieces, -0.22, 0.18) if pieces else 1.0
    entries = jax.random.normal(stream_key, shape, jnp.float32) * width * gain
    return jnp.minimum(jnp.maximum(entries, -bound), bound).astype(kind)


def setup_inputs(seed: int = 0) -> dict:
    key_of = jax.random.split(jax.random.key(seed), 7)
    return {
        "query_in": draw_query_in(jax.random.fold_in(key_of[6], 71), 0),
        "key_in": draw_key_in(jax.random.fold_in(key_of[6], 71), 0),
        "value_input": scatter_about(key_of[2], (BATCH_COUNT, SEQUENCE_LENGTH, KEY_VALUE_HEADS * HEAD_SIZE), 1.0, 4.0, ((0, 8), (1, 64))),
        "output_gradient": scatter_about(key_of[3], (BATCH_COUNT, SEQUENCE_LENGTH, QUERY_HEADS * HEAD_SIZE), 1.0, 5.0, ((0, 8), (1, 64))),
        "doc_ids": draw_doc_ids(jax.random.fold_in(key_of[6], 71), 0),
        "query_bias": scatter_about(key_of[5], (QUERY_HEADS * HEAD_SIZE,), 0.5, 2.0, (), jnp.float32),
    }


def reference(query_in, key_in, value_input, output_gradient, doc_ids, query_bias):
    score_scale = 1.0 / math.sqrt(HEAD_SIZE)
    padding_rows = (WB - 1) * BLK
    block_count = SEQUENCE_LENGTH // BLK

    def one_sequence(inputs):
        query_seq, key_sequence, value_sequence, gradient_sequence, docs_seq = inputs
        rounded_length = lax.optimization_barrier((query_seq.astype(jnp.float32) + query_bias).astype(jnp.bfloat16))
        query_rows = rounded_length.astype(jnp.float32).reshape(SEQUENCE_LENGTH, KEY_VALUE_HEADS, GROUP_SIZE, HEAD_SIZE)
        padded_keys = jnp.pad(key_sequence.astype(jnp.float32).reshape(SEQUENCE_LENGTH, KEY_VALUE_HEADS, HEAD_SIZE), ((padding_rows, 0), (0, 0), (0, 0)))
        padded_values = jnp.pad(value_sequence.astype(jnp.float32).reshape(SEQUENCE_LENGTH, KEY_VALUE_HEADS, HEAD_SIZE), ((padding_rows, 0), (0, 0), (0, 0)))
        gradient_list = gradient_sequence.astype(jnp.float32).reshape(SEQUENCE_LENGTH, KEY_VALUE_HEADS, GROUP_SIZE, HEAD_SIZE)
        docs_padded = jnp.pad(docs_seq, (padding_rows, 0), constant_values=-1)

        def block_step(running, block_index):
            key_accumulator, value_accumulator = running
            start = (block_index * BLK).astype(jnp.int32)
            query_block = lax.dynamic_slice_in_dim(query_rows, start, BLK, 0)
            grad_block = lax.dynamic_slice_in_dim(gradient_list, start, BLK, 0)
            query_docs = lax.dynamic_slice_in_dim(docs_seq, start, BLK, 0)
            key_block = lax.dynamic_slice_in_dim(padded_keys, start, WB * BLK, 0)
            value_block = lax.dynamic_slice_in_dim(padded_values, start, WB * BLK, 0)
            key_docs = lax.dynamic_slice_in_dim(docs_padded, start, WB * BLK, 0)
            query_pos = start + jnp.arange(BLK, dtype=jnp.int32)
            key_pos = start - padding_rows + jnp.arange(WB * BLK, dtype=jnp.int32)
            allowed = (key_pos[None, :] >= 0) & (key_pos[None, :] <= query_pos[:, None])
            allowed = allowed & (query_pos[:, None] // BLK - key_pos[None, :] // BLK < WB)
            allowed = allowed & (query_docs[:, None] == key_docs[None, :])
            scores = jnp.einsum('qgnd,kgd->gnqk', query_block, key_block) * score_scale
            scores = jnp.where(allowed[None, None], scores, -jnp.inf)
            row_max = lax.optimization_barrier(jnp.max(scores, axis=-1, keepdims=True))
            log_total = row_max + jnp.log(lax.optimization_barrier(jnp.sum(jnp.exp(scores - row_max), axis=-1, keepdims=True)))
            attend = jnp.exp(scores - log_total)
            attended = jnp.einsum('gnqk,kgd->qgnd', attend, value_block).astype(jnp.bfloat16)
            row_dot = jnp.einsum('qgnd,qgnd->gnq', grad_block, attended.astype(jnp.float32))
            grad_prob = jnp.einsum('qgnd,kgd->gnqk', grad_block, value_block)
            grad_score = lax.optimization_barrier((attend * (grad_prob - row_dot[..., None])).astype(jnp.bfloat16)).astype(jnp.float32)
            query_grad = jnp.einsum('gnqk,kgd->qgnd', grad_score, key_block) * score_scale
            key_grad = jnp.einsum('gnqk,qgnd->kgd', grad_score, query_block) * score_scale
            weight_bf = lax.optimization_barrier(attend.astype(jnp.bfloat16)).astype(jnp.float32)
            value_grad = jnp.einsum('gnqk,qgnd->kgd', weight_bf, grad_block)
            key_accumulator = lax.dynamic_update_slice_in_dim(key_accumulator, lax.dynamic_slice_in_dim(key_accumulator, start, WB * BLK, 0) + key_grad, start, 0)
            value_accumulator = lax.dynamic_update_slice_in_dim(value_accumulator, lax.dynamic_slice_in_dim(value_accumulator, start, WB * BLK, 0) + value_grad, start, 0)
            return ((key_accumulator, value_accumulator), (attended, query_grad))
        zero_filled = jnp.zeros((padding_rows + SEQUENCE_LENGTH, KEY_VALUE_HEADS, HEAD_SIZE), jnp.float32)
        (key_accumulator, value_accumulator), (attended_blocks, query_blocks) = lax.scan(block_step, (zero_filled, zero_filled), jnp.arange(block_count, dtype=jnp.int32))
        attended = attended_blocks.reshape(SEQUENCE_LENGTH, QUERY_HEADS * HEAD_SIZE)
        query_grad = query_blocks.reshape(SEQUENCE_LENGTH, QUERY_HEADS * HEAD_SIZE)
        key_gradient = key_accumulator[padding_rows:].reshape(SEQUENCE_LENGTH, KEY_VALUE_HEADS * HEAD_SIZE).astype(jnp.bfloat16)
        value_gradient = value_accumulator[padding_rows:].reshape(SEQUENCE_LENGTH, KEY_VALUE_HEADS * HEAD_SIZE).astype(jnp.bfloat16)
        return (attended, query_grad.astype(jnp.bfloat16), key_gradient, value_gradient, lax.optimization_barrier(jnp.sum(query_grad, axis=0)))
    results = lax.map(one_sequence, (query_in, key_in, value_input, output_gradient, doc_ids))
    grad_bias = lax.optimization_barrier(jnp.sum(results[4], axis=0))
    return (results[0], results[1], results[2], results[3], grad_bias)
```

```python
import math

import jax
import jax.numpy as jnp
from jax import lax
from jax.experimental import pallas as pl
from jax.experimental.pallas import tpu as pltpu
from jax.sharding import PartitionSpec as P

QUERY_HEADS = 14
GROUPS = 2
PER = 7
D = 128
BLK = 128
NX = 4
NZ = 16
NDP = 8
LEVELS = 4
QW = PER * BLK
LV = NX * BLK
PACK = 2 * BLK + 16
SCALE = 1.0 / math.sqrt(D)
SCALE2 = SCALE * math.log2(math.e)
NEG = -1e30
TILES = ((0, 256), (256, 256), (512, 256), (768, 128))
MESH = pl.DeviceIdType.MESH
F32 = jnp.float32
BF16 = jnp.bfloat16


def dot(a, b):
    return jnp.dot(a, b, preferred_element_type=F32)


def kernel(
    q_ref, k_ref, v_ref, do_ref, doc_ref, bias_ref,
    att_ref, gq_ref, gk_ref, gv_ref, gb_ref,
    kv, pen, qs, qt, dos, dot_t, probs, dsc, mlev, mrow, lrow, ot, dqt, fac,
    own, pout, xret, z2r, csend, crecv, lvl0,
    bdp, bx, bz,
    zs, zr, xs, xr, xs2, xr2, zs2, zr2, cs, cr, bs, br,
):
    ctx = lax.axis_index("ctx")
    dp = lax.axis_index("dp")
    z = ctx // NX
    x = ctx % NX

    def at(dz, dx):
        return {"ctx": ((z + dz + NZ) % NZ) * NX + (x + dx + NX) % NX}

    def at_dp(k):
        return {"dp": (dp + k) % NDP}

    barrier = pltpu.get_barrier_semaphore()
    for k in range(1, NZ):
        pl.semaphore_signal(barrier, inc=1, device_id=at(k, 0), device_id_type=MESH)
    for k in range(1, NX):
        pl.semaphore_signal(barrier, inc=1, device_id=at(0, k), device_id_type=MESH)
    for k in range(1, NDP):
        pl.semaphore_signal(barrier, inc=1, device_id=at_dp(k), device_id_type=MESH)

    def remote(src, dst, send, recv, where):
        return pltpu.make_async_remote_copy(
            src_ref=src, dst_ref=dst, send_sem=send, recv_sem=recv,
            device_id=where, device_id_type=MESH,
        )

    def slot(g, s):
        return kv.at[g, s, pl.ds(0, PACK if g == 0 else 2 * BLK)]

    def z_copy(g, l):
        return remote(slot(g, 4 * l), slot(g, 4 * l + 4), zs.at[g, l], zr.at[g, l], at(1, 0))

    def x_copy(g, l, r):
        return remote(slot(g, 4 * l), slot(g, 4 * l + r), xs.at[g, l, r - 1], xr.at[g, l, r - 1], at(0, r))

    def far_copy(g, r):
        return remote(slot(g, 16), slot(g, r), xs.at[g, 0, r - 1], xr.at[g, 0, r - 1], at(0, r))

    def z2_copy(g, l):
        return remote(slot(g, 4 * l - 2), slot(g, 4 * l + 2), xs.at[g, l, 1], xr.at[g, l, 1], at(1, 0))

    def xret_copy(g, l, r):
        return remote(pout.at[g, 4 * l + r], xret.at[g, l, r - 1], xs2.at[g, l, r - 1], xr2.at[g, l, r - 1], at(0, -r))

    def z2ret_copy(g, l):
        return remote(pout.at[g, 4 * l + 2], z2r.at[g, l - 2], zs2.at[g, l - 2], zr2.at[g, l - 2], at(-1, 0))

    def chain_copy(g, l):
        return remote(csend.at[g, l - 1], crecv.at[g, l - 1], cs.at[g, l - 1], cr.at[g, l - 1], at(-1, 0))

    docs = doc_ref[...].astype(F32)
    for g in range(GROUPS):
        kv[g, 0, 0:BLK, :] = k_ref[:, g * D : (g + 1) * D]
        kv[g, 0, BLK : 2 * BLK, :] = v_ref[:, g * D : (g + 1) * D]
    kv[0, 0, 2 * BLK : PACK, :] = jnp.broadcast_to(docs, (16, BLK)).astype(BF16)

    pl.semaphore_wait(barrier, NZ - 1 + NX - 1 + NDP - 1)

    def start_in(g):
        z_copy(g, 0).start()
        for r in range(1, NX):
            @pl.when(x + r < NX)
            def _(r=r):
                x_copy(g, 0, r).start()

    def service_in(g, l):
        z_copy(g, l - 1).wait_recv()
        if l < 4:
            z_copy(g, l).start()
            for r in (1, 2, 3) if l == 1 else (1, 3):
                x_copy(g, l, r).start()
        else:
            for r in range(1, NX):
                @pl.when(x + r >= NX)
                def _(r=r):
                    far_copy(g, r).start()

    def service_two(g, l):
        x_copy(g, l, 2).wait_recv()
        z2_copy(g, l + 1).start()

    def wait_level(g, l):
        for r in range(1, NX):
            if r == 2 and l in (1, 2):
                continue
            x_copy(g, l, r).wait_recv()

    def prepare():
        for h in range(QUERY_HEADS):
            g, c = h // PER, (h % PER) * BLK
            cols = slice(h * D, (h + 1) * D)
            qh = (q_ref[:, cols].astype(F32) + bias_ref[:, cols]).astype(BF16)
            qs[g, c : c + BLK, :] = qh
            qt[g, :, c : c + BLK] = qh.T
            dh = do_ref[:, cols]
            dos[g, c : c + BLK, :] = dh
            dot_t[g, :, c : c + BLK] = dh.T

    def penalties(l):
        key = lax.broadcasted_iota(jnp.int32, (BLK, BLK), 0).astype(F32)
        for r in range(NX):
            s = 4 * l + r
            kd = kv[0, s, 2 * BLK : PACK, :].astype(F32)[0:1, :]
            zeros = jnp.sum(1.0 - kd, axis=1, keepdims=True)
            limit = docs * zeros
            if l > 0:
                bad = (z < l).astype(F32)
            elif r > 0:
                bad = ((x < r) & (z < 4)).astype(F32)
            else:
                bad = None
            if bad is not None:
                limit = jnp.maximum(limit, bad * float(BLK))
            out = key < limit
            if s == 0:
                out = out | (key > lax.broadcasted_iota(jnp.int32, (BLK, BLK), 1).astype(F32))
            pen[s] = jnp.where(out, NEG, 0.0)

    def level_keys(g, l):
        return kv[g, 4 * l : 4 * l + 4, 0:BLK, :].reshape(LV, D)

    def level_values(g, l):
        return kv[g, 4 * l : 4 * l + 4, BLK : 2 * BLK, :].reshape(LV, D)

    def forward_level(g, l, first):
        keys = level_keys(g, l)
        values_t = level_values(g, l).T
        pn = pen[4 * l : 4 * l + 4].reshape(LV, BLK)
        for c, w in TILES:
            cols = slice(c, c + w)
            s = dot(keys, qt[g, :, cols]) * SCALE2
            s = s + (jnp.concatenate([pn, pn], axis=1) if w == 256 else pn)
            m = jnp.max(s, axis=0, keepdims=True)
            if not first:
                before = mrow[0:1, cols]
                m = jnp.maximum(m, before)
            p = jnp.exp2(s - m)
            total = jnp.sum(p, axis=0, keepdims=True)
            pb = p.astype(BF16)
            probs[l, :, cols] = pb
            o = dot(values_t, pb)
            if not first:
                shrink = jnp.exp2(before - m)
                total = total + lrow[0:1, cols] * shrink
                o = o + ot[:, cols] * shrink
            ot[:, cols] = o
            lrow[0:1, cols] = total
            mrow[0:1, cols] = m
            mlev[l, 0:1, cols] = m

    def normalise(g):
        inverse = 1.0 / lrow[0:1, :]
        for l in range(LEVELS):
            fac[l, 0:1, :] = jnp.exp2(mlev[l, 0:1, :] - mrow[0:1, :]) * inverse
        for j in range(PER):
            cols = slice(j * BLK, (j + 1) * BLK)
            h = g * PER + j
            att_t = ot[:, cols] * inverse[:, cols]
            rounded = att_t.astype(BF16)
            att_ref[:, h * D : (h + 1) * D] = rounded.T
            fac[4, 0:1, cols] = jnp.sum(
                rounded.astype(F32) * dot_t[g, :, cols].astype(F32), axis=0, keepdims=True
            )

    def backward_level(g, l, first):
        keys_t = level_keys(g, l).T
        values = level_values(g, l)
        for c, w in TILES:
            cols = slice(c, c + w)
            dpr = dot(values, dot_t[g, :, cols])
            pn = probs[l, :, cols].astype(F32) * fac[l, 0:1, cols]
            probs[l, :, cols] = pn.astype(BF16)
            ds = (pn * (dpr - fac[4, 0:1, cols])).astype(BF16)
            dsc[:, cols] = ds
            dq = dot(keys_t, ds)
            dqt[:, cols] = dq if first else dqt[:, cols] + dq
        dk = dot(dsc[...], qs[g]) * SCALE
        dv = dot(probs[l], dos[g])
        own[g, l, 0:BLK, :] = dk[0:BLK]
        own[g, l, BLK:, :] = dv[0:BLK]
        for r in range(1, NX):
            rows = slice(r * BLK, (r + 1) * BLK)
            pout[g, 4 * l + r, 0:BLK, :] = dk[rows].astype(BF16)
            pout[g, 4 * l + r, BLK:, :] = dv[rows].astype(BF16)

    def send_back(g, l):
        for r in (1, 2, 3) if l == 0 else (1, 3):
            xret_copy(g, l, r).start()
        if l == 3:
            z2ret_copy(g, 3).start()

    def two_back(g, l):
        z2ret_copy(g, l + 1).wait_recv()
        pout[g, 4 * l + 2] = (pout[g, 4 * l + 2].astype(F32) + z2r[g, l - 1].astype(F32)).astype(BF16)
        if l == 2:
            z2ret_copy(g, 2).start()
        else:
            xret_copy(g, 1, 2).start()

    def chain_first(g):
        near = own[g, 0]
        far = jnp.zeros((2 * BLK, D), F32)
        for r in range(1, NX):
            xret_copy(g, 0, r).wait_recv()
            here = (x + r < NX).astype(F32)
            got = xret[g, 0, r - 1].astype(F32)
            near = near + got * here
            far = far + got * (1.0 - here)
        lvl0[g] = near
        csend[g, 3] = far.astype(BF16)
        chain_copy(g, 4).start()

    def chain_step(g, l):
        total = own[g, l]
        for r in (1, 2, 3) if l == 1 else (1, 3):
            xret_copy(g, l, r).wait_recv()
            total = total + xret[g, l, r - 1].astype(F32)
        chain_copy(g, l + 1).wait_recv()
        csend[g, l - 1] = (total + crecv[g, l].astype(F32)).astype(BF16)
        chain_copy(g, l).start()

    def chain_last(g):
        chain_copy(g, 1).wait_recv()
        total = lvl0[g] + crecv[g, 0].astype(F32)
        gk_ref[:, g * D : (g + 1) * D] = total[0:BLK].astype(BF16)
        gv_ref[:, g * D : (g + 1) * D] = total[BLK:].astype(BF16)

    def finish_queries(g):
        for j in range(PER):
            h = g * PER + j
            dq = (dqt[:, j * BLK : (j + 1) * BLK] * SCALE).T
            gq_ref[:, h * D : (h + 1) * D] = dq.astype(BF16)
            bdp[dp, h : h + 1, :] = jnp.sum(dq, axis=0, keepdims=True)

    def bias_copy(buf, me, k, sem, where):
        return remote(buf.at[me], buf.at[me], bs.at[sem], br.at[sem], where)

    def bias_stage(buf, me, count, base, where):
        for k in range(1, count):
            bias_copy(buf, me, k, base + k, where(k)).start()

    def bias_sum(buf, me, count, base, where):
        for k in range(1, count):
            bias_copy(buf, me, k, base + k, where(k)).wait_recv()
        return jnp.sum(buf[...], axis=0)

    stages = (
        (bdp, dp, NDP, 0, at_dp),
        (bx, x, NX, NDP, lambda k: at(0, k)),
        (bz, z, NZ, NDP + NX, lambda k: at(k, 0)),
    )

    order = (1, 2, 3, 0)
    back = (0, 3, 2, 1)
    start_in(0)
    prepare()
    service_in(0, 1)
    service_in(0, 2)
    service_two(0, 1)
    for i, l in enumerate(order):
        if i == 1:
            service_two(0, 2)
        wait_level(0, l)
        penalties(l)
        forward_level(0, l, i == 0)
        if i == 0:
            service_in(0, 3)
        if i == 1:
            service_in(0, 4)
            start_in(1)
    normalise(0)
    service_in(1, 1)
    backward_level(0, 0, True)
    send_back(0, 0)
    service_in(1, 2)
    service_two(1, 1)
    backward_level(0, 3, False)
    send_back(0, 3)
    service_in(1, 3)
    service_two(1, 2)
    backward_level(0, 2, False)
    send_back(0, 2)
    two_back(0, 2)
    chain_first(0)
    service_in(1, 4)
    backward_level(0, 1, False)
    send_back(0, 1)
    two_back(0, 1)
    finish_queries(0)
    chain_step(0, 3)
    for i, l in enumerate(order):
        wait_level(1, l)
        forward_level(1, l, i == 0)
        if i == 0:
            chain_step(0, 2)
        if i == 1:
            chain_step(0, 1)
        if i == 2:
            chain_last(0)
    normalise(1)
    backward_level(1, 0, True)
    send_back(1, 0)
    backward_level(1, 3, False)
    send_back(1, 3)
    backward_level(1, 2, False)
    send_back(1, 2)
    two_back(1, 2)
    chain_first(1)
    backward_level(1, 1, False)
    send_back(1, 1)
    two_back(1, 1)
    bdp[dp, QUERY_HEADS:16, :] = jnp.zeros((2, D), F32)
    finish_queries(1)
    bias_stage(*stages[0])
    chain_step(1, 3)
    bx[x] = bias_sum(*stages[0])
    bias_stage(*stages[1])
    chain_step(1, 2)
    bz[z] = bias_sum(*stages[1])
    bias_stage(*stages[2])
    chain_step(1, 1)
    chain_last(1)
    gb_ref[...] = bias_sum(*stages[2])

    for g in range(GROUPS):
        for l in range(4):
            z_copy(g, l).wait_send()
            chain_copy(g, l + 1).wait_send()
            for r in range(1, NX):
                x_copy(g, l, r).wait_send()
                if not (r == 2 and l in (2, 3)):
                    xret_copy(g, l, r).wait_send()
        for l in (2, 3):
            z2ret_copy(g, l).wait_send()
    for buf, me, count, base, where in stages:
        for k in range(1, count):
            bias_copy(buf, me, k, base + k, where(k)).wait_send()


def local(query_in, key_in, value_input, output_gradient, doc_ids, query_bias):
    vm = pl.BlockSpec(memory_space=pltpu.VMEM)
    dma = pltpu.SemaphoreType.DMA
    V = pltpu.VMEM
    att, gq, gk, gv, gb = pl.pallas_call(
        kernel,
        out_shape=(
            jax.ShapeDtypeStruct((BLK, QUERY_HEADS * D), BF16),
            jax.ShapeDtypeStruct((BLK, QUERY_HEADS * D), BF16),
            jax.ShapeDtypeStruct((BLK, GROUPS * D), BF16),
            jax.ShapeDtypeStruct((BLK, GROUPS * D), BF16),
            jax.ShapeDtypeStruct((16, D), F32),
        ),
        in_specs=[vm] * 6,
        out_specs=[vm] * 5,
        scratch_shapes=[
            V((GROUPS, 17, PACK, D), BF16),
            V((16, BLK, BLK), F32),
            V((GROUPS, QW, D), BF16),
            V((GROUPS, D, QW), BF16),
            V((GROUPS, QW, D), BF16),
            V((GROUPS, D, QW), BF16),
            V((LEVELS, LV, QW), BF16),
            V((LV, QW), BF16),
            V((LEVELS, 8, QW), F32),
            V((8, QW), F32),
            V((8, QW), F32),
            V((D, QW), F32),
            V((D, QW), F32),
            V((5, 8, QW), F32),
            V((GROUPS, LEVELS, 2 * BLK, D), F32),
            V((GROUPS, 16, 2 * BLK, D), BF16),
            V((GROUPS, LEVELS, 3, 2 * BLK, D), BF16),
            V((GROUPS, 2, 2 * BLK, D), BF16),
            V((GROUPS, 4, 2 * BLK, D), BF16),
            V((GROUPS, 4, 2 * BLK, D), BF16),
            V((GROUPS, 2 * BLK, D), F32),
            V((NDP, 16, D), F32),
            V((NX, 16, D), F32),
            V((NZ, 16, D), F32),
            dma((GROUPS, 4)), dma((GROUPS, 4)),
            dma((GROUPS, 4, 3)), dma((GROUPS, 4, 3)),
            dma((GROUPS, 4, 3)), dma((GROUPS, 4, 3)),
            dma((GROUPS, 2)), dma((GROUPS, 2)),
            dma((GROUPS, 4)), dma((GROUPS, 4)),
            dma((NDP + NX + NZ,)), dma((NDP + NX + NZ,)),
        ],
        compiler_params=pltpu.CompilerParams(
            collective_id=0, has_side_effects=True, vmem_limit_bytes=56 << 20
        ),
    )(
        query_in[0], key_in[0], value_input[0], output_gradient[0], doc_ids, query_bias[None],
    )
    return (att[None], gq[None], gk[None], gv[None], gb[:QUERY_HEADS].reshape(QUERY_HEADS * D))


def solution(mesh):
    rows = P("dp", "ctx", None)
    return jax.shard_map(
        local,
        mesh=mesh,
        in_specs=(rows, rows, rows, rows, P("dp", "ctx"), P()),
        out_specs=(rows, rows, rows, rows, P()),
        check_vma=False,
    )
```

```python
import math

import jax
import jax.numpy as jnp
from jax import lax
from jax.experimental import pallas as pl
from jax.experimental.pallas import tpu as pltpu
from jax.sharding import PartitionSpec as P

QUERY_HEADS = 14
GROUPS = 2
PER = 7
D = 128
BLK = 128
NX = 4
NZ = 16
NDP = 8
LEVELS = 4
QW = PER * BLK
LV = NX * BLK
PACK = 2 * BLK + 16
SCALE = 1.0 / math.sqrt(D)
SCALE2 = SCALE * math.log2(math.e)
NEG = -1e30
TILES = ((0, 256), (256, 256), (512, 256), (768, 128))
MESH = pl.DeviceIdType.MESH
F32 = jnp.float32
BF16 = jnp.bfloat16


def turn(g, l):
    return 1 if l == 2 or (l == 3 and g == 1) else -1


def dot(a, b):
    return jnp.dot(a, b, preferred_element_type=F32)


def kernel(
    q_hbm, k_hbm, v_hbm, do_hbm, doc_ref, bias_ref,
    att_ref, gq_ref, gk_ref, gv_ref, gb_ref,
    q_ref, do_ref, kv, pen, qs, qt, dos, dot_t, probs, dsc, mlev, mrow, lrow, ot, dqt, fac,
    own, pout, xret, csend, crecv, lvl0,
    bdp, bx, bz,
    ins, zs, zr, xs, xr, xs2, xr2, cs, cr, bs, br,
):
    ctx = lax.axis_index("ctx")
    dp = lax.axis_index("dp")
    z = ctx // NX
    x = ctx % NX

    def at(dz, dx):
        return {"ctx": ((z + dz + NZ) % NZ) * NX + (x + dx + NX) % NX}

    def at_dp(k):
        return {"dp": (dp + k) % NDP}

    barrier = pltpu.get_barrier_semaphore()
    for k in range(1, NZ):
        pl.semaphore_signal(barrier, inc=1, device_id=at(k, 0), device_id_type=MESH)
    for k in range(1, NX):
        pl.semaphore_signal(barrier, inc=1, device_id=at(0, k), device_id_type=MESH)
    for k in range(1, NDP):
        pl.semaphore_signal(barrier, inc=1, device_id=at_dp(k), device_id_type=MESH)

    def remote(src, dst, send, recv, where):
        return pltpu.make_async_remote_copy(
            src_ref=src, dst_ref=dst, send_sem=send, recv_sem=recv,
            device_id=where, device_id_type=MESH,
        )

    def slot(g, s):
        return kv.at[g, s, pl.ds(0, PACK if g == 0 else 2 * BLK)]

    def z_copy(g, l):
        source = 4 if l == 3 else 4 * l - 4
        return remote(slot(g, source), slot(g, 4 * l), zs.at[g, l - 1], zr.at[g, l - 1], at(2 if l == 3 else 1, 0))

    def x_copy(g, l, r):
        return remote(slot(g, 4 * l), slot(g, 4 * l + r), xs.at[g, l, r - 1], xr.at[g, l, r - 1], at(0, r))

    def far_copy(g, r):
        return remote(slot(g, 16), slot(g, r), xs.at[g, 0, r - 1], xr.at[g, 0, r - 1], at(0, r))

    def two_copy(g, l):
        d = turn(g, l)
        source = 4 * l + (1 if d > 0 else 3)
        return remote(slot(g, source), slot(g, 4 * l + 2), xs.at[g, l, 1], xr.at[g, l, 1], at(0, d))

    def two_back(g, l):
        return remote(pout.at[g, 4 * l + 2], xret.at[g, l, 1], xs2.at[g, l, 1], xr2.at[g, l, 1], at(0, -turn(g, l)))

    def xret_copy(g, l, r):
        return remote(pout.at[g, 4 * l + r], xret.at[g, l, r - 1], xs2.at[g, l, r - 1], xr2.at[g, l, r - 1], at(0, -r))

    def chain_copy(g, l):
        return remote(csend.at[g, l - 1], crecv.at[g, l - 1], cs.at[g, l - 1], cr.at[g, l - 1], at(-2 if l == 3 else -1, 0))

    def fetch(i, src, dst):
        return pltpu.make_async_copy(src, dst, ins.at[i])

    fetches = [fetch(0, q_hbm, q_ref), fetch(1, do_hbm, do_ref)]
    for g in range(GROUPS):
        lanes = pl.ds(g * D, D)
        fetches.append(fetch(2 + g, k_hbm.at[:, lanes], kv.at[g, 0, pl.ds(0, BLK)]))
        fetches.append(fetch(4 + g, v_hbm.at[:, lanes], kv.at[g, 0, pl.ds(BLK, BLK)]))
    for f in fetches:
        f.start()
    docs = doc_ref[...].astype(F32)
    kv[0, 0, 2 * BLK : PACK, :] = jnp.broadcast_to(docs, (16, BLK)).astype(BF16)
    for f in fetches[2:]:
        f.wait()

    def start_in(g):
        z_copy(g, 1).start()
        for r in range(1, NX):
            @pl.when(x + r < NX)
            def _(r=r):
                x_copy(g, 0, r).start()

    def service_in(g, l):
        z_copy(g, l).wait_recv()
        if l == 1:
            z_copy(g, 2).start()
            z_copy(g, 3).start()
        if l == 3:
            z_copy(g, 4).start()
        if l < 4:
            x_copy(g, l, 1).start()
            x_copy(g, l, 3).start()
        else:
            for r in range(1, NX):
                @pl.when(x + r >= NX)
                def _(r=r):
                    far_copy(g, r).start()

    def service_two(g, l):
        x_copy(g, l, 1 if turn(g, l) > 0 else 3).wait_recv()
        two_copy(g, l).start()

    def wait_level(g, l):
        if l == 0:
            for r in range(1, NX):
                x_copy(g, l, r).wait_recv()
        else:
            x_copy(g, l, 3 if turn(g, l) > 0 else 1).wait_recv()
            two_copy(g, l).wait_recv()

    def prepare():
        for h in range(QUERY_HEADS):
            g, c = h // PER, (h % PER) * BLK
            cols = slice(h * D, (h + 1) * D)
            qh = (q_ref[:, cols].astype(F32) + bias_ref[cols].reshape(1, D)).astype(BF16)
            qs[g, c : c + BLK, :] = qh
            qt[g, :, c : c + BLK] = qh.T
            dh = do_ref[:, cols]
            dos[g, c : c + BLK, :] = dh
            dot_t[g, :, c : c + BLK] = dh.T

    def penalties(l):
        key = lax.broadcasted_iota(jnp.int32, (BLK, BLK), 0).astype(F32)
        for r in range(NX):
            s = 4 * l + r
            kd = kv[0, s, 2 * BLK : PACK, :].astype(F32)[0:1, :]
            zeros = jnp.sum(1.0 - kd, axis=1, keepdims=True)
            limit = docs * zeros
            if l > 0:
                bad = (z < l).astype(F32)
            elif r > 0:
                bad = ((x < r) & (z < 4)).astype(F32)
            else:
                bad = None
            if bad is not None:
                limit = jnp.maximum(limit, bad * float(BLK))
            out = key < limit
            if s == 0:
                out = out | (key > lax.broadcasted_iota(jnp.int32, (BLK, BLK), 1).astype(F32))
            pen[s] = jnp.where(out, NEG, 0.0)

    def level_keys(g, l):
        return kv[g, 4 * l : 4 * l + 4, 0:BLK, :].reshape(LV, D)

    def level_values(g, l):
        return kv[g, 4 * l : 4 * l + 4, BLK : 2 * BLK, :].reshape(LV, D)

    def forward_level(g, l, first):
        keys = level_keys(g, l)
        values_t = level_values(g, l).T
        pn = pen[4 * l : 4 * l + 4].reshape(LV, BLK)
        for c, w in TILES:
            cols = slice(c, c + w)
            s = dot(keys, qt[g, :, cols]) * SCALE2
            s = s + (jnp.concatenate([pn, pn], axis=1) if w == 256 else pn)
            m = jnp.max(s, axis=0, keepdims=True)
            if not first:
                before = mrow[g, 0:1, cols]
                m = jnp.maximum(m, before)
            p = jnp.exp2(s - m)
            total = jnp.sum(p, axis=0, keepdims=True)
            pb = p.astype(BF16)
            probs[g, l, :, cols] = pb
            o = dot(values_t, pb)
            if not first:
                shrink = jnp.exp2(before - m)
                total = total + lrow[g, 0:1, cols] * shrink
                o = o + ot[g, :, cols] * shrink
            ot[g, :, cols] = o
            lrow[g, 0:1, cols] = total
            mrow[g, 0:1, cols] = m
            mlev[g, l, 0:1, cols] = m

    def normalise(g):
        inverse = 1.0 / lrow[g, 0:1, :]
        for l in range(LEVELS):
            fac[g, l, 0:1, :] = jnp.exp2(mlev[g, l, 0:1, :] - mrow[g, 0:1, :]) * inverse
        for j in range(PER):
            cols = slice(j * BLK, (j + 1) * BLK)
            h = g * PER + j
            att_t = ot[g, :, cols] * inverse[:, cols]
            rounded = att_t.astype(BF16)
            att_ref[:, h * D : (h + 1) * D] = rounded.T
            fac[g, 4, 0:1, cols] = jnp.sum(
                rounded.astype(F32) * dot_t[g, :, cols].astype(F32), axis=0, keepdims=True
            )

    def backward_queries(g, l, first):
        keys_t = level_keys(g, l).T
        values = level_values(g, l)
        for c, w in TILES:
            cols = slice(c, c + w)
            dpr = dot(values, dot_t[g, :, cols])
            pn = probs[g, l, :, cols].astype(F32) * fac[g, l, 0:1, cols]
            probs[g, l, :, cols] = pn.astype(BF16)
            ds = (pn * (dpr - fac[g, 4, 0:1, cols])).astype(BF16)
            dsc[g, :, cols] = ds
            dq = dot(keys_t, ds)
            dqt[g, :, cols] = dq if first else dqt[g, :, cols] + dq

    def backward_keys(g, l):
        dk = dot(dsc[g], qs[g]) * SCALE
        dv = dot(probs[g, l], dos[g])
        own[g, l, 0:BLK, :] = dk[0:BLK]
        own[g, l, BLK:, :] = dv[0:BLK]
        for r in range(1, NX):
            rows = slice(r * BLK, (r + 1) * BLK)
            pout[g, 4 * l + r, 0:BLK, :] = dk[rows].astype(BF16)
            pout[g, 4 * l + r, BLK:, :] = dv[rows].astype(BF16)

        if l == 0:
            for r in range(1, NX):
                xret_copy(g, l, r).start()
        else:
            two_back(g, l).start()
            xret_copy(g, l, 3 if turn(g, l) > 0 else 1).start()

    def merge(g, l):
        r = 1 if turn(g, l) > 0 else 3
        two_back(g, l).wait_recv()
        pout[g, 4 * l + r] = (pout[g, 4 * l + r].astype(F32) + xret[g, l, 1].astype(F32)).astype(BF16)
        xret_copy(g, l, r).start()

    def gather(g, l, total):
        for r in (1, 3):
            xret_copy(g, l, r).wait_recv()
            total = total + xret[g, l, r - 1].astype(F32)
        return total

    def chain(g, l):
        if l == 4:
            near = own[g, 0]
            total = jnp.zeros((2 * BLK, D), F32)
            for r in range(1, NX):
                xret_copy(g, 0, r).wait_recv()
                here = (x + r < NX).astype(F32)
                got = xret[g, 0, r - 1].astype(F32)
                near = near + got * here
                total = total + got * (1.0 - here)
            lvl0[g] = near
        else:
            total = gather(g, l, own[g, l])
        for below in {4: (), 3: (4,), 2: (), 1: (2, 3)}[l]:
            chain_copy(g, below).wait_recv()
            total = total + crecv[g, below - 1].astype(F32)
        csend[g, l - 1] = total.astype(BF16)
        chain_copy(g, l).start()

    def chain_last(g):
        chain_copy(g, 1).wait_recv()
        total = lvl0[g] + crecv[g, 0].astype(F32)
        gk_ref[:, g * D : (g + 1) * D] = total[0:BLK].astype(BF16)
        gv_ref[:, g * D : (g + 1) * D] = total[BLK:].astype(BF16)

    def finish_queries(g):
        for j in range(PER):
            h = g * PER + j
            dq = (dqt[g, :, j * BLK : (j + 1) * BLK] * SCALE).T
            gq_ref[:, h * D : (h + 1) * D] = dq.astype(BF16)
            bdp[dp, h : h + 1, :] = jnp.sum(dq, axis=0, keepdims=True)

    def bias_copy(buf, me, k, sem, where):
        return remote(buf.at[me], buf.at[me], bs.at[sem], br.at[sem], where)

    def bias_stage(buf, me, count, base, where):
        for k in range(1, count):
            bias_copy(buf, me, k, base + k, where(k)).start()

    def bias_sum(buf, me, count, base, where):
        for k in range(1, count):
            bias_copy(buf, me, k, base + k, where(k)).wait_recv()
        return jnp.sum(buf[...], axis=0)

    stages = (
        (bdp, dp, NDP, 0, at_dp),
        (bx, x, NX, NDP, lambda k: at(0, k)),
        (bz, z, NZ, NDP + NX, lambda k: at(k, 0)),
    )

    def forward(g, l, first=False):
        wait_level(g, l)
        if g == 0:
            penalties(l)
        forward_level(g, l, first)

    def backward(g, l, first=False):
        backward_queries(g, l, first)
        backward_keys(g, l)

    pl.semaphore_wait(barrier, NZ - 1 + NX - 1 + NDP - 1)
    start_in(0)
    start_in(1)
    for f in fetches[:2]:
        f.wait()
    prepare()
    service_in(0, 1)
    service_in(1, 1)
    service_two(0, 1)
    service_in(0, 2)
    service_in(0, 3)
    service_two(1, 1)
    service_in(1, 2)
    service_in(1, 3)
    forward(0, 1, True)
    service_in(0, 4)
    service_two(0, 2)
    service_two(0, 3)
    forward(1, 1, True)
    service_in(1, 4)
    service_two(1, 2)
    service_two(1, 3)
    forward(0, 2)
    forward(0, 3)
    forward(0, 0)
    normalise(0)
    backward(0, 0, True)
    forward(1, 2)
    backward(0, 3)
    forward(1, 3)
    chain(0, 4)
    forward(1, 0)
    normalise(1)
    merge(0, 3)
    backward(1, 0, True)
    backward(0, 2)
    chain(0, 3)
    backward(1, 3)
    merge(0, 2)
    chain(1, 4)
    backward(0, 1)
    merge(1, 3)
    finish_queries(0)
    backward(1, 2)
    chain(0, 2)
    merge(0, 1)
    backward_queries(1, 1, False)
    bdp[dp, QUERY_HEADS:16, :] = jnp.zeros((2, D), F32)
    finish_queries(1)
    bias_stage(*stages[0])
    backward_keys(1, 1)
    merge(1, 2)
    chain(1, 3)
    bx[x] = bias_sum(*stages[0])
    bias_stage(*stages[1])
    merge(1, 1)
    chain(0, 1)
    chain(1, 2)
    bz[z] = bias_sum(*stages[1])
    bias_stage(*stages[2])
    chain(1, 1)
    chain_last(0)
    chain_last(1)
    gb_ref[...] = bias_sum(*stages[2])

    for g in range(GROUPS):
        for l in range(4):
            z_copy(g, l + 1).wait_send()
            chain_copy(g, l + 1).wait_send()
            for r in range(1, NX):
                if r == 2 and l > 0:
                    two_copy(g, l).wait_send()
                    two_back(g, l).wait_send()
                else:
                    x_copy(g, l, r).wait_send()
                    xret_copy(g, l, r).wait_send()
    for buf, me, count, base, where in stages:
        for k in range(1, count):
            bias_copy(buf, me, k, base + k, where(k)).wait_send()


def hand_over(att, gq, gk, gv, gb, att_out, gq_out, gk_out, gv_out, gb_out, sem):
    pairs = ((att, att_out), (gq, gq_out), (gk, gk_out), (gv, gv_out))
    copies = [pltpu.make_async_copy(a, b.at[0], sem.at[i]) for i, (a, b) in enumerate(pairs)]
    for c in copies:
        c.start()
    for h in range(QUERY_HEADS):
        gb_out[h * D : (h + 1) * D] = gb[h, :]
    for c in copies:
        c.wait()


def local(query_in, key_in, value_input, output_gradient, doc_ids, query_bias):
    vm = pl.BlockSpec(memory_space=pltpu.VMEM)
    anyspace = pl.BlockSpec(memory_space=pl.ANY)
    dma = pltpu.SemaphoreType.DMA
    V = pltpu.VMEM
    att, gq, gk, gv, gb = pl.pallas_call(
        kernel,
        out_shape=(
            jax.ShapeDtypeStruct((BLK, QUERY_HEADS * D), BF16),
            jax.ShapeDtypeStruct((BLK, QUERY_HEADS * D), BF16),
            jax.ShapeDtypeStruct((BLK, GROUPS * D), BF16),
            jax.ShapeDtypeStruct((BLK, GROUPS * D), BF16),
            jax.ShapeDtypeStruct((16, D), F32),
        ),
        in_specs=[anyspace] * 4 + [vm] * 2,
        out_specs=[vm] * 5,
        scratch_shapes=[
            V((BLK, QUERY_HEADS * D), BF16),
            V((BLK, QUERY_HEADS * D), BF16),
            V((GROUPS, 17, PACK, D), BF16),
            V((16, BLK, BLK), F32),
            V((GROUPS, QW, D), BF16),
            V((GROUPS, D, QW), BF16),
            V((GROUPS, QW, D), BF16),
            V((GROUPS, D, QW), BF16),
            V((GROUPS, LEVELS, LV, QW), BF16),
            V((GROUPS, LV, QW), BF16),
            V((GROUPS, LEVELS, 8, QW), F32),
            V((GROUPS, 8, QW), F32),
            V((GROUPS, 8, QW), F32),
            V((GROUPS, D, QW), F32),
            V((GROUPS, D, QW), F32),
            V((GROUPS, 5, 8, QW), F32),
            V((GROUPS, LEVELS, 2 * BLK, D), F32),
            V((GROUPS, 16, 2 * BLK, D), BF16),
            V((GROUPS, LEVELS, 3, 2 * BLK, D), BF16),
            V((GROUPS, 4, 2 * BLK, D), BF16),
            V((GROUPS, 4, 2 * BLK, D), BF16),
            V((GROUPS, 2 * BLK, D), F32),
            V((NDP, 16, D), F32),
            V((NX, 16, D), F32),
            V((NZ, 16, D), F32),
            dma((6,)),
            dma((GROUPS, 4)), dma((GROUPS, 4)),
            dma((GROUPS, 4, 3)), dma((GROUPS, 4, 3)),
            dma((GROUPS, 4, 3)), dma((GROUPS, 4, 3)),
            dma((GROUPS, 4)), dma((GROUPS, 4)),
            dma((NDP + NX + NZ,)), dma((NDP + NX + NZ,)),
        ],
        compiler_params=pltpu.CompilerParams(
            collective_id=0, has_side_effects=True, vmem_limit_bytes=56 << 20
        ),
    )(
        query_in[0], key_in[0], value_input[0], output_gradient[0], doc_ids, query_bias,
    )
    return pl.pallas_call(
        hand_over,
        out_shape=(
            jax.ShapeDtypeStruct((1, BLK, QUERY_HEADS * D), BF16),
            jax.ShapeDtypeStruct((1, BLK, QUERY_HEADS * D), BF16),
            jax.ShapeDtypeStruct((1, BLK, GROUPS * D), BF16),
            jax.ShapeDtypeStruct((1, BLK, GROUPS * D), BF16),
            jax.ShapeDtypeStruct((QUERY_HEADS * D,), F32),
        ),
        in_specs=[vm] * 5,
        out_specs=[anyspace] * 4 + [vm],
        scratch_shapes=[dma((4,))],
    )(att, gq, gk, gv, gb)


def solution(mesh):
    rows = P("dp", "ctx", None)
    return jax.shard_map(
        local,
        mesh=mesh,
        in_specs=(rows, rows, rows, rows, P("dp", "ctx"), P()),
        out_specs=(rows, rows, rows, rows, P()),
        check_vma=False,
    )
```

```python
import math

import jax
import jax.numpy as jnp
from jax import lax
from jax.experimental import pallas as pl
from jax.experimental.pallas import tpu as pltpu
from jax.sharding import PartitionSpec as P

QUERY_HEADS = 14
GROUPS = 2
PER = 7
D = 128
BLK = 128
NX = 4
NZ = 16
NDP = 8
LEVELS = 4
QW = PER * BLK
LV = NX * BLK
PACK = 2 * BLK + 16
SCALE = 1.0 / math.sqrt(D)
SCALE2 = SCALE * math.log2(math.e)
NEG = -1e30
TILES = ((0, 256), (256, 256), (512, 256), (768, 128))
MESH = pl.DeviceIdType.MESH
F32 = jnp.float32
BF16 = jnp.bfloat16


def turn(g, l):
    return 1 if l == 2 or (l == 3 and g == 1) else -1


def straight(g, l):
    return g == 0 and l in (1, 2)


def dot(a, b):
    return jnp.dot(a, b, preferred_element_type=F32)


def kernel(
    q_hbm, k_hbm, v_hbm, do_hbm, doc_ref, bias_ref,
    att_ref, gq_ref, gk_ref, gv_ref, gb_ref,
    q_ref, do_ref, kv, pen, qs, qt, dos, dot_t, probs, dsc, mlev, mrow, lrow, ot, dqt, fac,
    own, pout, xret, csend, crecv, lvl0,
    bdp, bx, bz,
    ins, zs, zr, xs, xr, xs2, xr2, cs, cr, bs, br,
):
    ctx = lax.axis_index("ctx")
    dp = lax.axis_index("dp")
    z = ctx // NX
    x = ctx % NX

    def at(dz, dx):
        return {"ctx": ((z + dz + NZ) % NZ) * NX + (x + dx + NX) % NX}

    def at_dp(k):
        return {"dp": (dp + k) % NDP}

    barrier = pltpu.get_barrier_semaphore()
    def greet(where):
        pl.semaphore_signal(barrier, inc=1, device_id=where, device_id_type=MESH)

    for k in (-1, 1, -2, 2):
        greet(at(k, 0))
    for k in range(1, NX):
        greet(at(0, k))
    for k in range(1, NDP):
        greet(at_dp(k))
    for k in range(3, NZ - 2):
        greet(at(k, 0))

    def remote(src, dst, send, recv, where):
        return pltpu.make_async_remote_copy(
            src_ref=src, dst_ref=dst, send_sem=send, recv_sem=recv,
            device_id=where, device_id_type=MESH,
        )

    def slot(g, s):
        return kv.at[g, s, pl.ds(0, PACK if g == 0 else 2 * BLK)]

    def z_copy(g, l):
        source = 4 if l == 3 else 4 * l - 4
        return remote(slot(g, source), slot(g, 4 * l), zs.at[g, l - 1], zr.at[g, l - 1], at(2 if l == 3 else 1, 0))

    def x_copy(g, l, r):
        return remote(slot(g, 4 * l), slot(g, 4 * l + r), xs.at[g, l, r - 1], xr.at[g, l, r - 1], at(0, r))

    def far_copy(g, r):
        return remote(slot(g, 16), slot(g, r), xs.at[g, 0, r - 1], xr.at[g, 0, r - 1], at(0, r))

    def two_copy(g, l):
        d = turn(g, l)
        source = 4 * l + (1 if d > 0 else 3)
        return remote(slot(g, source), slot(g, 4 * l + 2), xs.at[g, l, 1], xr.at[g, l, 1], at(0, d))

    def two_back(g, l):
        return remote(pout.at[g, 4 * l + 2], xret.at[g, l, 1], xs2.at[g, l, 1], xr2.at[g, l, 1], at(0, -turn(g, l)))

    def xret_copy(g, l, r):
        return remote(pout.at[g, 4 * l + r], xret.at[g, l, r - 1], xs2.at[g, l, r - 1], xr2.at[g, l, r - 1], at(0, -r))

    def chain_copy(g, l):
        return remote(csend.at[g, l - 1], crecv.at[g, l - 1], cs.at[g, l - 1], cr.at[g, l - 1], at(-2 if l == 3 else -1, 0))

    def fetch(i, src, dst):
        return pltpu.make_async_copy(src, dst, ins.at[i])

    fetches = [fetch(0, q_hbm, q_ref), fetch(1, do_hbm, do_ref)]
    for g in range(GROUPS):
        lanes = pl.ds(g * D, D)
        fetches.append(fetch(2 + g, k_hbm.at[:, lanes], kv.at[g, 0, pl.ds(0, BLK)]))
        fetches.append(fetch(4 + g, v_hbm.at[:, lanes], kv.at[g, 0, pl.ds(BLK, BLK)]))
    for f in fetches:
        f.start()
    docs = doc_ref[...].astype(F32)
    kv[0, 0, 2 * BLK : PACK, :] = jnp.broadcast_to(docs, (16, BLK)).astype(BF16)
    for f in fetches[2:]:
        f.wait()

    def near_in(g):
        for r in range(1, NX):
            @pl.when(x + r < NX)
            def _(r=r):
                x_copy(g, 0, r).start()

    def along_z(g, l):
        if l == 1:
            z_copy(g, 3).start()
            z_copy(g, 2).start()
        if l == 3:
            z_copy(g, 4).start()

    def along_x(g, l):
        if l < 4:
            x_copy(g, l, 1).start()
            x_copy(g, l, 3).start()
            if straight(g, l):
                x_copy(g, l, 2).start()
        else:
            for r in range(1, NX):
                @pl.when(x + r >= NX)
                def _(r=r):
                    far_copy(g, r).start()

    def service_in(g, l):
        z_copy(g, l).wait_recv()
        along_z(g, l)
        along_x(g, l)

    def service_two(g, l):
        x_copy(g, l, 1 if turn(g, l) > 0 else 3).wait_recv()
        two_copy(g, l).start()

    def wait_level(g, l):
        if l == 0 or straight(g, l):
            for r in range(1, NX):
                x_copy(g, l, r).wait_recv()
        else:
            x_copy(g, l, 3 if turn(g, l) > 0 else 1).wait_recv()
            two_copy(g, l).wait_recv()

    def prepare():
        for h in range(QUERY_HEADS):
            g, c = h // PER, (h % PER) * BLK
            cols = slice(h * D, (h + 1) * D)
            qh = (q_ref[:, cols].astype(F32) + bias_ref[cols].reshape(1, D)).astype(BF16)
            qs[g, c : c + BLK, :] = qh
            qt[g, :, c : c + BLK] = qh.T
            dh = do_ref[:, cols]
            dos[g, c : c + BLK, :] = dh
            dot_t[g, :, c : c + BLK] = dh.T

    def penalties(l):
        key = lax.broadcasted_iota(jnp.int32, (BLK, BLK), 0).astype(F32)
        for r in range(NX):
            s = 4 * l + r
            kd = kv[0, s, 2 * BLK : PACK, :].astype(F32)[0:1, :]
            zeros = jnp.sum(1.0 - kd, axis=1, keepdims=True)
            limit = docs * zeros
            if l > 0:
                bad = (z < l).astype(F32)
            elif r > 0:
                bad = ((x < r) & (z < 4)).astype(F32)
            else:
                bad = None
            if bad is not None:
                limit = jnp.maximum(limit, bad * float(BLK))
            out = key < limit
            if s == 0:
                out = out | (key > lax.broadcasted_iota(jnp.int32, (BLK, BLK), 1).astype(F32))
            pen[s] = jnp.where(out, NEG, 0.0)

    def level_keys(g, l):
        return kv[g, 4 * l : 4 * l + 4, 0:BLK, :].reshape(LV, D)

    def level_values(g, l):
        return kv[g, 4 * l : 4 * l + 4, BLK : 2 * BLK, :].reshape(LV, D)

    def forward_level(g, l, first):
        keys = level_keys(g, l)
        values_t = level_values(g, l).T
        pn = pen[4 * l : 4 * l + 4].reshape(LV, BLK)
        for c, w in TILES:
            cols = slice(c, c + w)
            s = dot(keys, qt[g, :, cols]) * SCALE2
            s = s + (jnp.concatenate([pn, pn], axis=1) if w == 256 else pn)
            m = jnp.max(s, axis=0, keepdims=True)
            if not first:
                before = mrow[g, 0:1, cols]
                m = jnp.maximum(m, before)
            p = jnp.exp2(s - m)
            total = jnp.sum(p, axis=0, keepdims=True)
            pb = p.astype(BF16)
            probs[g, l, :, cols] = pb
            o = dot(values_t, pb)
            if not first:
                shrink = jnp.exp2(before - m)
                total = total + lrow[g, 0:1, cols] * shrink
                o = o + ot[g, :, cols] * shrink
            ot[g, :, cols] = o
            lrow[g, 0:1, cols] = total
            mrow[g, 0:1, cols] = m
            mlev[g, l, 0:1, cols] = m

    def normalise(g):
        inverse = 1.0 / lrow[g, 0:1, :]
        for l in range(LEVELS):
            fac[g, l, 0:1, :] = jnp.exp2(mlev[g, l, 0:1, :] - mrow[g, 0:1, :]) * inverse
        for j in range(PER):
            cols = slice(j * BLK, (j + 1) * BLK)
            h = g * PER + j
            att_t = ot[g, :, cols] * inverse[:, cols]
            rounded = att_t.astype(BF16)
            att_ref[:, h * D : (h + 1) * D] = rounded.T
            fac[g, 4, 0:1, cols] = jnp.sum(
                rounded.astype(F32) * dot_t[g, :, cols].astype(F32), axis=0, keepdims=True
            )

    def backward_queries(g, l, first):
        keys_t = level_keys(g, l).T
        values = level_values(g, l)
        for c, w in TILES:
            cols = slice(c, c + w)
            dpr = dot(values, dot_t[g, :, cols])
            pn = probs[g, l, :, cols].astype(F32) * fac[g, l, 0:1, cols]
            probs[g, l, :, cols] = pn.astype(BF16)
            ds = (pn * (dpr - fac[g, 4, 0:1, cols])).astype(BF16)
            dsc[g, l, :, cols] = ds
            dq = dot(keys_t, ds)
            dqt[g, :, cols] = dq if first else dqt[g, :, cols] + dq

    def backward_keys(g, l):
        dk = dot(dsc[g, l], qs[g]) * SCALE
        dv = dot(probs[g, l], dos[g])
        own[g, l, 0:BLK, :] = dk[0:BLK]
        own[g, l, BLK:, :] = dv[0:BLK]
        for r in range(1, NX):
            rows = slice(r * BLK, (r + 1) * BLK)
            pout[g, 4 * l + r, 0:BLK, :] = dk[rows].astype(BF16)
            pout[g, 4 * l + r, BLK:, :] = dv[rows].astype(BF16)

        if l < 3:
            for r in range(1, NX):
                xret_copy(g, l, r).start()
        else:
            two_back(g, l).start()
            xret_copy(g, l, 3 if turn(g, l) > 0 else 1).start()

    def merge(g, l):
        r = 1 if turn(g, l) > 0 else 3
        two_back(g, l).wait_recv()
        pout[g, 4 * l + r] = (pout[g, 4 * l + r].astype(F32) + xret[g, l, 1].astype(F32)).astype(BF16)
        xret_copy(g, l, r).start()

    def gather(g, l, total):
        for r in (1, 3) if l == 3 else (1, 2, 3):
            xret_copy(g, l, r).wait_recv()
            total = total + xret[g, l, r - 1].astype(F32)
        return total

    def chain(g, l):
        if l == 4:
            near = own[g, 0]
            total = jnp.zeros((2 * BLK, D), F32)
            for r in range(1, NX):
                xret_copy(g, 0, r).wait_recv()
                here = (x + r < NX).astype(F32)
                got = xret[g, 0, r - 1].astype(F32)
                near = near + got * here
                total = total + got * (1.0 - here)
            lvl0[g] = near
        else:
            total = gather(g, l, own[g, l])
        for below in {4: (), 3: (4,), 2: (), 1: (2, 3)}[l]:
            chain_copy(g, below).wait_recv()
            total = total + crecv[g, below - 1].astype(F32)
        csend[g, l - 1] = total.astype(BF16)
        chain_copy(g, l).start()

    def chain_last(g):
        chain_copy(g, 1).wait_recv()
        total = lvl0[g] + crecv[g, 0].astype(F32)
        gk_ref[:, g * D : (g + 1) * D] = total[0:BLK].astype(BF16)
        gv_ref[:, g * D : (g + 1) * D] = total[BLK:].astype(BF16)

    def finish_queries(g):
        for j in range(PER):
            h = g * PER + j
            dq = (dqt[g, :, j * BLK : (j + 1) * BLK] * SCALE).T
            gq_ref[:, h * D : (h + 1) * D] = dq.astype(BF16)

    def bias_rows():
        lane = lax.broadcasted_iota(jnp.int32, (D, BLK), 1)
        columns = jnp.zeros((D, BLK), F32)
        for h in range(QUERY_HEADS):
            c = (h % PER) * BLK
            total = jnp.sum(dqt[h // PER, :, c : c + BLK], axis=1, keepdims=True) * SCALE
            columns = jnp.where(lane == h, total, columns)
        bdp[dp] = columns.T[0:16]

    def bias_copy(buf, me, k, sem, where):
        return remote(buf.at[me], buf.at[me], bs.at[sem], br.at[sem], where)

    def bias_stage(buf, me, count, base, where):
        for k in range(1, count):
            bias_copy(buf, me, k, base + k, where(k)).start()

    def bias_sum(buf, me, count, base, where):
        for k in range(1, count):
            bias_copy(buf, me, k, base + k, where(k)).wait_recv()
        return jnp.sum(buf[...], axis=0)

    stages = (
        (bdp, dp, NDP, 0, at_dp),
        (bx, x, NX, NDP, lambda k: at(0, k)),
        (bz, z, NZ, NDP + NX, lambda k: at(k, 0)),
    )

    def forward(g, l, first=False):
        wait_level(g, l)
        if g == 0:
            penalties(l)
        forward_level(g, l, first)

    def backward(g, l, first=False):
        backward_queries(g, l, first)
        backward_keys(g, l)

    pl.semaphore_wait(barrier, NZ - 1 + NX - 1 + NDP - 1)
    z_copy(0, 1).start()
    z_copy(1, 1).start()
    near_in(0)
    for f in fetches[:2]:
        f.wait()
    prepare()
    service_in(0, 1)
    z_copy(1, 1).wait_recv()
    along_x(1, 1)
    near_in(1)
    service_in(0, 3)
    service_in(0, 2)
    along_z(1, 1)
    service_two(1, 1)
    forward(0, 1, True)
    service_two(0, 3)
    service_in(0, 4)
    forward(1, 1, True)
    service_in(1, 3)
    service_in(1, 2)
    forward(0, 2)
    forward(0, 3)
    service_two(1, 3)
    service_two(1, 2)
    service_in(1, 4)
    forward(0, 0)
    normalise(0)
    backward(0, 0, True)
    forward(1, 2)
    backward(0, 3)
    forward(1, 3)
    chain(0, 4)
    forward(1, 0)
    normalise(1)
    backward(1, 0, True)
    merge(0, 3)
    backward(1, 3)
    backward_queries(0, 2, False)
    backward_queries(0, 1, False)
    chain(1, 4)
    backward_queries(1, 2, False)
    backward_queries(1, 1, False)
    bias_rows()
    bias_stage(*stages[0])
    backward_keys(0, 2)
    chain(0, 3)
    merge(1, 3)
    backward_keys(1, 2)
    backward_keys(0, 1)
    backward_keys(1, 1)
    bx[x] = bias_sum(*stages[0])
    bias_stage(*stages[1])
    chain(1, 3)
    chain(0, 2)
    chain(1, 2)
    finish_queries(0)
    bz[z] = bias_sum(*stages[1])
    bias_stage(*stages[2])
    finish_queries(1)
    chain(0, 1)
    chain(1, 1)
    chain_last(0)
    chain_last(1)
    gb_ref[...] = bias_sum(*stages[2])

    for g in range(GROUPS):
        for l in range(4):
            z_copy(g, l + 1).wait_send()
            chain_copy(g, l + 1).wait_send()
            for r in range(1, NX):
                if r == 2 and l > 0 and not straight(g, l):
                    two_copy(g, l).wait_send()
                else:
                    x_copy(g, l, r).wait_send()
                if r == 2 and l == 3:
                    two_back(g, l).wait_send()
                else:
                    xret_copy(g, l, r).wait_send()
    for buf, me, count, base, where in stages:
        for k in range(1, count):
            bias_copy(buf, me, k, base + k, where(k)).wait_send()


def hand_over(att, gq, gk, gv, gb, att_out, gq_out, gk_out, gv_out, gb_out, sem):
    pairs = ((att, att_out), (gq, gq_out), (gk, gk_out), (gv, gv_out))
    copies = [pltpu.make_async_copy(a, b.at[0], sem.at[i]) for i, (a, b) in enumerate(pairs)]
    for c in copies:
        c.start()
    for h in range(QUERY_HEADS):
        gb_out[h * D : (h + 1) * D] = gb[h, :]
    for c in copies:
        c.wait()


def local(query_in, key_in, value_input, output_gradient, doc_ids, query_bias):
    vm = pl.BlockSpec(memory_space=pltpu.VMEM)
    anyspace = pl.BlockSpec(memory_space=pl.ANY)
    dma = pltpu.SemaphoreType.DMA
    V = pltpu.VMEM
    att, gq, gk, gv, gb = pl.pallas_call(
        kernel,
        out_shape=(
            jax.ShapeDtypeStruct((BLK, QUERY_HEADS * D), BF16),
            jax.ShapeDtypeStruct((BLK, QUERY_HEADS * D), BF16),
            jax.ShapeDtypeStruct((BLK, GROUPS * D), BF16),
            jax.ShapeDtypeStruct((BLK, GROUPS * D), BF16),
            jax.ShapeDtypeStruct((16, D), F32),
        ),
        in_specs=[anyspace] * 4 + [vm] * 2,
        out_specs=[vm] * 5,
        scratch_shapes=[
            V((BLK, QUERY_HEADS * D), BF16),
            V((BLK, QUERY_HEADS * D), BF16),
            V((GROUPS, 17, PACK, D), BF16),
            V((16, BLK, BLK), F32),
            V((GROUPS, QW, D), BF16),
            V((GROUPS, D, QW), BF16),
            V((GROUPS, QW, D), BF16),
            V((GROUPS, D, QW), BF16),
            V((GROUPS, LEVELS, LV, QW), BF16),
            V((GROUPS, LEVELS, LV, QW), BF16),
            V((GROUPS, LEVELS, 8, QW), F32),
            V((GROUPS, 8, QW), F32),
            V((GROUPS, 8, QW), F32),
            V((GROUPS, D, QW), F32),
            V((GROUPS, D, QW), F32),
            V((GROUPS, 5, 8, QW), F32),
            V((GROUPS, LEVELS, 2 * BLK, D), F32),
            V((GROUPS, 16, 2 * BLK, D), BF16),
            V((GROUPS, LEVELS, 3, 2 * BLK, D), BF16),
            V((GROUPS, 4, 2 * BLK, D), BF16),
            V((GROUPS, 4, 2 * BLK, D), BF16),
            V((GROUPS, 2 * BLK, D), F32),
            V((NDP, 16, D), F32),
            V((NX, 16, D), F32),
            V((NZ, 16, D), F32),
            dma((6,)),
            dma((GROUPS, 4)), dma((GROUPS, 4)),
            dma((GROUPS, 4, 3)), dma((GROUPS, 4, 3)),
            dma((GROUPS, 4, 3)), dma((GROUPS, 4, 3)),
            dma((GROUPS, 4)), dma((GROUPS, 4)),
            dma((NDP + NX + NZ,)), dma((NDP + NX + NZ,)),
        ],
        compiler_params=pltpu.CompilerParams(
            collective_id=0, has_side_effects=True, vmem_limit_bytes=56 << 20
        ),
    )(
        query_in[0], key_in[0], value_input[0], output_gradient[0], doc_ids, query_bias,
    )
    return pl.pallas_call(
        hand_over,
        out_shape=(
            jax.ShapeDtypeStruct((1, BLK, QUERY_HEADS * D), BF16),
            jax.ShapeDtypeStruct((1, BLK, QUERY_HEADS * D), BF16),
            jax.ShapeDtypeStruct((1, BLK, GROUPS * D), BF16),
            jax.ShapeDtypeStruct((1, BLK, GROUPS * D), BF16),
            jax.ShapeDtypeStruct((QUERY_HEADS * D,), F32),
        ),
        in_specs=[vm] * 5,
        out_specs=[anyspace] * 4 + [vm],
        scratch_shapes=[dma((4,))],
    )(att, gq, gk, gv, gb)


def solution(mesh):
    rows = P("dp", "ctx", None)
    return jax.shard_map(
        local,
        mesh=mesh,
        in_specs=(rows, rows, rows, rows, P("dp", "ctx"), P()),
        out_specs=(rows, rows, rows, rows, P()),
        check_vma=False,
    )
```

```python
import math

import jax
import jax.numpy as jnp
from jax import lax
from jax.experimental import pallas as pl
from jax.experimental.pallas import tpu as pltpu
from jax.sharding import PartitionSpec as P

QUERY_HEADS = 14
GROUPS = 2
PER = 7
D = 128
BLK = 128
NX = 4
NZ = 16
NDP = 8
LEVELS = 4
QW = PER * BLK
LV = NX * BLK
PACK = 2 * BLK + 16
SCALE = 1.0 / math.sqrt(D)
SCALE2 = SCALE * math.log2(math.e)
NEG = -1e30
TILES = ((0, 256), (256, 256), (512, 256), (768, 128))
MESH = pl.DeviceIdType.MESH
F32 = jnp.float32
BF16 = jnp.bfloat16


def turn(g, l):
    return 1 if l == 2 or (l == 3 and g == 1) else -1


def straight(g, l):
    return g == 0 and l in (1, 2)


def dot(a, b):
    return jnp.dot(a, b, preferred_element_type=F32)


def kernel(
    q_hbm, k_hbm, v_hbm, do_hbm, doc_ref, bias_ref,
    att_ref, gq_ref, gk_ref, gv_ref, gb_ref,
    q_ref, do_ref, kv, pen, qs, qt, dos, dot_t, probs, dsc, mlev, mrow, lrow, ot, dqt, fac,
    own, pout, xret, csend, crecv, lvl0,
    bdp, bx, bz,
    ins, zs, zr, xs, xr, xs2, xr2, cs, cr, bs, br,
):
    ctx = lax.axis_index("ctx")
    dp = lax.axis_index("dp")
    z = ctx // NX
    x = ctx % NX

    def at(dz, dx):
        return {"ctx": ((z + dz + NZ) % NZ) * NX + (x + dx + NX) % NX}

    def at_dp(k):
        return {"dp": (dp + k) % NDP}

    barrier = pltpu.get_barrier_semaphore()
    def greet(where):
        pl.semaphore_signal(barrier, inc=1, device_id=where, device_id_type=MESH)

    for k in (-1, 1, -2, 2):
        greet(at(k, 0))
    for k in range(1, NX):
        greet(at(0, k))
    for k in range(1, NDP):
        greet(at_dp(k))
    for k in range(3, NZ - 2):
        greet(at(k, 0))

    def remote(src, dst, send, recv, where):
        return pltpu.make_async_remote_copy(
            src_ref=src, dst_ref=dst, send_sem=send, recv_sem=recv,
            device_id=where, device_id_type=MESH,
        )

    def slot(g, s):
        return kv.at[g, s, pl.ds(0, PACK if g == 0 else 2 * BLK)]

    def z_copy(g, l):
        source = 4 if l == 3 else 4 * l - 4
        return remote(slot(g, source), slot(g, 4 * l), zs.at[g, l - 1], zr.at[g, l - 1], at(2 if l == 3 else 1, 0))

    def x_copy(g, l, r):
        return remote(slot(g, 4 * l), slot(g, 4 * l + r), xs.at[g, l, r - 1], xr.at[g, l, r - 1], at(0, r))

    def far_copy(g, r):
        return remote(slot(g, 16), slot(g, r), xs.at[g, 0, r - 1], xr.at[g, 0, r - 1], at(0, r))

    def two_copy(g, l):
        d = turn(g, l)
        source = 4 * l + (1 if d > 0 else 3)
        return remote(slot(g, source), slot(g, 4 * l + 2), xs.at[g, l, 1], xr.at[g, l, 1], at(0, d))

    def two_back(g, l):
        return remote(pout.at[g, 4 * l + 2], xret.at[g, l, 1], xs2.at[g, l, 1], xr2.at[g, l, 1], at(0, -turn(g, l)))

    def xret_copy(g, l, r):
        return remote(pout.at[g, 4 * l + r], xret.at[g, l, r - 1], xs2.at[g, l, r - 1], xr2.at[g, l, r - 1], at(0, -r))

    def chain_copy(g, l):
        return remote(csend.at[g, l - 1], crecv.at[g, l - 1], cs.at[g, l - 1], cr.at[g, l - 1], at(-2 if l == 3 else -1, 0))

    def fetch(i, src, dst):
        return pltpu.make_async_copy(src, dst, ins.at[i])

    fetches = [fetch(0, q_hbm, q_ref), fetch(1, do_hbm, do_ref)]
    for g in range(GROUPS):
        lanes = pl.ds(g * D, D)
        fetches.append(fetch(2 + g, k_hbm.at[:, lanes], kv.at[g, 0, pl.ds(0, BLK)]))
        fetches.append(fetch(4 + g, v_hbm.at[:, lanes], kv.at[g, 0, pl.ds(BLK, BLK)]))
    for f in fetches:
        f.start()
    docs = doc_ref[...].astype(F32)
    kv[0, 0, 2 * BLK : PACK, :] = jnp.broadcast_to(docs, (16, BLK)).astype(BF16)
    for f in fetches[2:]:
        f.wait()

    def near_in(g):
        for r in range(1, NX):
            @pl.when(x + r < NX)
            def _(r=r):
                x_copy(g, 0, r).start()

    def along_z(g, l):
        if l == 1:
            z_copy(g, 3).start()
            z_copy(g, 2).start()
        if l == 3:
            z_copy(g, 4).start()

    def along_x(g, l):
        if l < 4:
            x_copy(g, l, 1).start()
            x_copy(g, l, 3).start()
            if straight(g, l):
                x_copy(g, l, 2).start()
        else:
            for r in range(1, NX):
                @pl.when(x + r >= NX)
                def _(r=r):
                    far_copy(g, r).start()

    def service_in(g, l):
        z_copy(g, l).wait_recv()
        along_z(g, l)
        along_x(g, l)

    def service_two(g, l):
        x_copy(g, l, 1 if turn(g, l) > 0 else 3).wait_recv()
        two_copy(g, l).start()

    def wait_level(g, l):
        if l == 0 or straight(g, l):
            for r in range(1, NX):
                x_copy(g, l, r).wait_recv()
        else:
            x_copy(g, l, 3 if turn(g, l) > 0 else 1).wait_recv()
            two_copy(g, l).wait_recv()

    def prepare():
        for h in range(QUERY_HEADS):
            g, c = h // PER, (h % PER) * BLK
            cols = slice(h * D, (h + 1) * D)
            qh = (q_ref[:, cols].astype(F32) + bias_ref[cols].reshape(1, D)).astype(BF16)
            qs[g, c : c + BLK, :] = qh
            qt[g, :, c : c + BLK] = qh.T
            dh = do_ref[:, cols]
            dos[g, c : c + BLK, :] = dh
            dot_t[g, :, c : c + BLK] = dh.T

    def penalties(l):
        key = lax.broadcasted_iota(jnp.int32, (BLK, BLK), 0).astype(F32)
        for r in range(NX):
            s = 4 * l + r
            kd = kv[0, s, 2 * BLK : PACK, :].astype(F32)[0:1, :]
            zeros = jnp.sum(1.0 - kd, axis=1, keepdims=True)
            limit = docs * zeros
            if l > 0:
                bad = (z < l).astype(F32)
            elif r > 0:
                bad = ((x < r) & (z < 4)).astype(F32)
            else:
                bad = None
            if bad is not None:
                limit = jnp.maximum(limit, bad * float(BLK))
            out = key < limit
            if s == 0:
                out = out | (key > lax.broadcasted_iota(jnp.int32, (BLK, BLK), 1).astype(F32))
            pen[s] = jnp.where(out, NEG, 0.0)

    def level_keys(g, l):
        return kv[g, 4 * l : 4 * l + 4, 0:BLK, :].reshape(LV, D)

    def level_values(g, l):
        return kv[g, 4 * l : 4 * l + 4, BLK : 2 * BLK, :].reshape(LV, D)

    def forward_level(g, l, first):
        keys = level_keys(g, l)
        values_t = level_values(g, l).T
        pn = pen[4 * l : 4 * l + 4].reshape(LV, BLK)
        for c, w in TILES:
            cols = slice(c, c + w)
            s = dot(keys, qt[g, :, cols]) * SCALE2
            s = s + (jnp.concatenate([pn, pn], axis=1) if w == 256 else pn)
            m = jnp.max(s, axis=0, keepdims=True)
            if not first:
                before = mrow[g, 0:1, cols]
                m = jnp.maximum(m, before)
            p = jnp.exp2(s - m)
            total = jnp.sum(p, axis=0, keepdims=True)
            pb = p.astype(BF16)
            probs[g, l, :, cols] = pb
            o = dot(values_t, pb)
            if not first:
                shrink = jnp.exp2(before - m)
                total = total + lrow[g, 0:1, cols] * shrink
                o = o + ot[g, :, cols] * shrink
            ot[g, :, cols] = o
            lrow[g, 0:1, cols] = total
            mrow[g, 0:1, cols] = m
            mlev[g, l, 0:1, cols] = m

    def normalise(g):
        inverse = 1.0 / lrow[g, 0:1, :]
        for l in range(LEVELS):
            fac[g, l, 0:1, :] = jnp.exp2(mlev[g, l, 0:1, :] - mrow[g, 0:1, :]) * inverse
        for j in range(PER):
            cols = slice(j * BLK, (j + 1) * BLK)
            h = g * PER + j
            att_t = ot[g, :, cols] * inverse[:, cols]
            rounded = att_t.astype(BF16)
            att_ref[:, h * D : (h + 1) * D] = rounded.T
            fac[g, 4, 0:1, cols] = jnp.sum(
                rounded.astype(F32) * dot_t[g, :, cols].astype(F32), axis=0, keepdims=True
            )

    def backward_queries(g, l, first):
        keys_t = level_keys(g, l).T
        values = level_values(g, l)
        for c, w in TILES:
            cols = slice(c, c + w)
            dpr = dot(values, dot_t[g, :, cols])
            pn = probs[g, l, :, cols].astype(F32) * fac[g, l, 0:1, cols]
            probs[g, l, :, cols] = pn.astype(BF16)
            ds = (pn * (dpr - fac[g, 4, 0:1, cols])).astype(BF16)
            dsc[g, l, :, cols] = ds
            dq = dot(keys_t, ds)
            dqt[g, :, cols] = dq if first else dqt[g, :, cols] + dq

    def backward_keys(g, l):
        dk = dot(dsc[g, l], qs[g]) * SCALE
        dv = dot(probs[g, l], dos[g])
        own[g, l, 0:BLK, :] = dk[0:BLK]
        own[g, l, BLK:, :] = dv[0:BLK]
        for r in range(1, NX):
            rows = slice(r * BLK, (r + 1) * BLK)
            pout[g, 4 * l + r, 0:BLK, :] = dk[rows].astype(BF16)
            pout[g, 4 * l + r, BLK:, :] = dv[rows].astype(BF16)

        if l < 3:
            for r in range(1, NX):
                xret_copy(g, l, r).start()
        else:
            two_back(g, l).start()
            xret_copy(g, l, 3 if turn(g, l) > 0 else 1).start()

    def merge(g, l):
        r = 1 if turn(g, l) > 0 else 3
        two_back(g, l).wait_recv()
        pout[g, 4 * l + r] = (pout[g, 4 * l + r].astype(F32) + xret[g, l, 1].astype(F32)).astype(BF16)
        xret_copy(g, l, r).start()

    def gather(g, l, total):
        for r in (1, 3) if l == 3 else (1, 2, 3):
            xret_copy(g, l, r).wait_recv()
            total = total + xret[g, l, r - 1].astype(F32)
        return total

    def chain(g, l):
        if l == 4:
            near = own[g, 0]
            total = jnp.zeros((2 * BLK, D), F32)
            for r in range(1, NX):
                xret_copy(g, 0, r).wait_recv()
                here = (x + r < NX).astype(F32)
                got = xret[g, 0, r - 1].astype(F32)
                near = near + got * here
                total = total + got * (1.0 - here)
            lvl0[g] = near
        else:
            total = gather(g, l, own[g, l])
        for below in {4: (), 3: (4,), 2: (), 1: (2, 3)}[l]:
            chain_copy(g, below).wait_recv()
            total = total + crecv[g, below - 1].astype(F32)
        csend[g, l - 1] = total.astype(BF16)
        chain_copy(g, l).start()

    def chain_last(g):
        chain_copy(g, 1).wait_recv()
        total = lvl0[g] + crecv[g, 0].astype(F32)
        gk_ref[:, g * D : (g + 1) * D] = total[0:BLK].astype(BF16)
        gv_ref[:, g * D : (g + 1) * D] = total[BLK:].astype(BF16)

    def finish_queries(g):
        for j in range(PER):
            h = g * PER + j
            dq = (dqt[g, :, j * BLK : (j + 1) * BLK] * SCALE).T
            gq_ref[:, h * D : (h + 1) * D] = dq.astype(BF16)

    def bias_rows():
        lane = lax.broadcasted_iota(jnp.int32, (D, BLK), 1)
        columns = jnp.zeros((D, BLK), F32)
        for h in range(QUERY_HEADS):
            c = (h % PER) * BLK
            total = jnp.sum(dqt[h // PER, :, c : c + BLK], axis=1, keepdims=True) * SCALE
            columns = jnp.where(lane == h, total, columns)
        bdp[dp] = columns.T[0:16]

    def bias_copy(buf, me, k, sem, where):
        return remote(buf.at[me], buf.at[me], bs.at[sem], br.at[sem], where)

    def bias_stage(buf, me, count, base, where):
        for k in range(1, count):
            bias_copy(buf, me, k, base + k, where(k)).start()

    def bias_sum(buf, me, count, base, where):
        for k in range(1, count):
            bias_copy(buf, me, k, base + k, where(k)).wait_recv()
        return jnp.sum(buf[...], axis=0)

    stages = (
        (bdp, dp, NDP, 0, at_dp),
        (bx, x, NX, NDP, lambda k: at(0, k)),
        (bz, z, NZ, NDP + NX, lambda k: at(k, 0)),
    )

    def forward(g, l, first=False):
        wait_level(g, l)
        if g == 0:
            penalties(l)
        forward_level(g, l, first)

    def backward(g, l, first=False):
        backward_queries(g, l, first)
        backward_keys(g, l)

    pl.semaphore_wait(barrier, NZ - 1 + NX - 1 + NDP - 1)
    z_copy(0, 1).start()
    z_copy(1, 1).start()
    near_in(0)
    for f in fetches[:2]:
        f.wait()
    prepare()
    service_in(0, 1)
    z_copy(1, 1).wait_recv()
    along_x(1, 1)
    near_in(1)
    service_in(0, 3)
    service_in(0, 2)
    along_z(1, 1)
    service_two(1, 1)
    forward(0, 1, True)
    service_two(0, 3)
    service_in(0, 4)
    forward(1, 1, True)
    service_in(1, 3)
    service_in(1, 2)
    forward(0, 2)
    forward(0, 3)
    service_two(1, 3)
    service_two(1, 2)
    service_in(1, 4)
    forward(0, 0)
    normalise(0)
    backward(0, 0, True)
    forward(1, 2)
    backward(0, 3)
    forward(1, 3)
    chain(0, 4)
    forward(1, 0)
    normalise(1)
    backward(1, 0, True)
    merge(0, 3)
    backward(1, 3)
    backward_queries(0, 2, False)
    backward_queries(0, 1, False)
    chain(1, 4)
    backward_queries(1, 2, False)
    backward_queries(1, 1, False)
    bias_rows()
    bias_stage(*stages[0])
    backward_keys(0, 2)
    chain(0, 3)
    merge(1, 3)
    backward_keys(1, 2)
    backward_keys(0, 1)
    backward_keys(1, 1)
    chain(1, 3)
    chain(0, 2)
    bx[x] = bias_sum(*stages[0])
    bias_stage(*stages[1])
    chain(1, 2)
    finish_queries(0)
    bz[z] = bias_sum(*stages[1])
    bias_stage(*stages[2])
    finish_queries(1)
    chain(0, 1)
    chain(1, 1)
    chain_last(0)
    chain_last(1)
    gb_ref[...] = bias_sum(*stages[2])

    for g in range(GROUPS):
        for l in range(4):
            z_copy(g, l + 1).wait_send()
            chain_copy(g, l + 1).wait_send()
            for r in range(1, NX):
                if r == 2 and l > 0 and not straight(g, l):
                    two_copy(g, l).wait_send()
                else:
                    x_copy(g, l, r).wait_send()
                if r == 2 and l == 3:
                    two_back(g, l).wait_send()
                else:
                    xret_copy(g, l, r).wait_send()
    for buf, me, count, base, where in stages:
        for k in range(1, count):
            bias_copy(buf, me, k, base + k, where(k)).wait_send()


def hand_over(att, gq, gk, gv, gb, att_out, gq_out, gk_out, gv_out, gb_out, sem):
    pairs = ((att, att_out), (gq, gq_out), (gk, gk_out), (gv, gv_out))
    copies = [pltpu.make_async_copy(a, b.at[0], sem.at[i]) for i, (a, b) in enumerate(pairs)]
    for c in copies:
        c.start()
    for h in range(QUERY_HEADS):
        gb_out[h * D : (h + 1) * D] = gb[h, :]
    for c in copies:
        c.wait()


def local(query_in, key_in, value_input, output_gradient, doc_ids, query_bias):
    vm = pl.BlockSpec(memory_space=pltpu.VMEM)
    anyspace = pl.BlockSpec(memory_space=pl.ANY)
    dma = pltpu.SemaphoreType.DMA
    V = pltpu.VMEM
    att, gq, gk, gv, gb = pl.pallas_call(
        kernel,
        out_shape=(
            jax.ShapeDtypeStruct((BLK, QUERY_HEADS * D), BF16),
            jax.ShapeDtypeStruct((BLK, QUERY_HEADS * D), BF16),
            jax.ShapeDtypeStruct((BLK, GROUPS * D), BF16),
            jax.ShapeDtypeStruct((BLK, GROUPS * D), BF16),
            jax.ShapeDtypeStruct((16, D), F32),
        ),
        in_specs=[anyspace] * 4 + [vm] * 2,
        out_specs=[vm] * 5,
        scratch_shapes=[
            V((BLK, QUERY_HEADS * D), BF16),
            V((BLK, QUERY_HEADS * D), BF16),
            V((GROUPS, 17, PACK, D), BF16),
            V((16, BLK, BLK), F32),
            V((GROUPS, QW, D), BF16),
            V((GROUPS, D, QW), BF16),
            V((GROUPS, QW, D), BF16),
            V((GROUPS, D, QW), BF16),
            V((GROUPS, LEVELS, LV, QW), BF16),
            V((GROUPS, LEVELS, LV, QW), BF16),
            V((GROUPS, LEVELS, 8, QW), F32),
            V((GROUPS, 8, QW), F32),
            V((GROUPS, 8, QW), F32),
            V((GROUPS, D, QW), F32),
            V((GROUPS, D, QW), F32),
            V((GROUPS, 5, 8, QW), F32),
            V((GROUPS, LEVELS, 2 * BLK, D), F32),
            V((GROUPS, 16, 2 * BLK, D), BF16),
            V((GROUPS, LEVELS, 3, 2 * BLK, D), BF16),
            V((GROUPS, 4, 2 * BLK, D), BF16),
            V((GROUPS, 4, 2 * BLK, D), BF16),
            V((GROUPS, 2 * BLK, D), F32),
            V((NDP, 16, D), F32),
            V((NX, 16, D), F32),
            V((NZ, 16, D), F32),
            dma((6,)),
            dma((GROUPS, 4)), dma((GROUPS, 4)),
            dma((GROUPS, 4, 3)), dma((GROUPS, 4, 3)),
            dma((GROUPS, 4, 3)), dma((GROUPS, 4, 3)),
            dma((GROUPS, 4)), dma((GROUPS, 4)),
            dma((NDP + NX + NZ,)), dma((NDP + NX + NZ,)),
        ],
        compiler_params=pltpu.CompilerParams(
            collective_id=0, has_side_effects=True, vmem_limit_bytes=56 << 20
        ),
    )(
        query_in[0], key_in[0], value_input[0], output_gradient[0], doc_ids, query_bias,
    )
    return pl.pallas_call(
        hand_over,
        out_shape=(
            jax.ShapeDtypeStruct((1, BLK, QUERY_HEADS * D), BF16),
            jax.ShapeDtypeStruct((1, BLK, QUERY_HEADS * D), BF16),
            jax.ShapeDtypeStruct((1, BLK, GROUPS * D), BF16),
            jax.ShapeDtypeStruct((1, BLK, GROUPS * D), BF16),
            jax.ShapeDtypeStruct((QUERY_HEADS * D,), F32),
        ),
        in_specs=[vm] * 5,
        out_specs=[anyspace] * 4 + [vm],
        scratch_shapes=[dma((4,))],
    )(att, gq, gk, gv, gb)


def solution(mesh):
    rows = P("dp", "ctx", None)
    return jax.shard_map(
        local,
        mesh=mesh,
        in_specs=(rows, rows, rows, rows, P("dp", "ctx"), P()),
        out_specs=(rows, rows, rows, rows, P()),
        check_vma=False,
    )
```
